32 devices in a mesh: row: 8 (over z, y), col: 4 (over x, core).
Axes of the slice: x: 2, y: 2, z: 4, core: 2. Of those that a mesh axis runs over, the one named last changes fastest.
Arguments:
- star_state: float32 [7, 65536], P(None, ('row', 'col')), as said below
- active_index: int32 [8192], P(('row', 'col')), may hold values from 0 to 2047, as said below
- neighbour_index: int32 [8192, 128], P(('row', 'col')), may hold values from 0 to 2047, as said below
- assignment: int32 [8192, 1], P(('row', 'col')), may hold values from 0 to 31, as said below
- start_state: float32 [6, 8192], P(None, ('row', 'col')), may hold values from -6 to 6
- old_derivs: float32 [6, 8192], P(None, ('row', 'col')), may hold values from -12 to 12
- step_size: float32 [8192], P(('row', 'col')), may hold values from 0.1 to 1
Outputs:
- corrected: float32 [6, 8192], P(None, ('row', 'col'))
- forces: float32 [12, 8192], P(None, ('row', 'col'))
The draws below stay inside these ranges and needn't reach their ends.
Inputs may be any that keep to these rules, and one draw needn't show every extreme that they name: `star_state`: row 6 (masses) is positive. `active_index`: within each aligned block of 256 entries (the active stars of one device) the entries are distinct. `neighbour_index`: the 128 entries of each row are distinct. `assignment`: within the rows of one device (aligned blocks of 256 rows) no device number appears more than 16 times, and some appears exactly 16 times.
All inputs are finite; a program needn't handle non-finite values.
Results may differ from the reference program's by a relative error of at most 0.000028.
Values sent between devices are 32-bit elements; how exact they have to be, the bound alone decides.
A program may use at most 192 MiB of HBM per device.

```python
import math
import jax
import jax.numpy as jnp
from jax import lax

ACT_DEV = 256
S_DEV = 2048
K = 128
NACT = 8192
NSTARS = 65536
MOST = 16
DEVICES = 32


def pick_distinct(pick_key, count):
    order = jax.random.permutation(pick_key, S_DEV)
    return order[:count].astype(jnp.int32)


def pick_with_top(pick_key, count):
    order = jax.random.permutation(pick_key, S_DEV).astype(jnp.int32)
    places = jnp.arange(S_DEV, dtype=jnp.int32)
    swapped = jnp.where(order == S_DEV - 1, order[0], jnp.where(places == 0, S_DEV - 1, order))
    return swapped[:count].astype(jnp.int32)


def layout(seed_key):
    keys = jax.random.split(seed_key, 6)
    slots_total = DEVICES * MOST
    hot_count = max(1, ACT_DEV // (4 * MOST))
    hot_order = jax.random.permutation(keys[0], DEVICES).astype(jnp.int32)
    is_hot = (hot_order < hot_count).astype(jnp.int32)
    slot_owner = jnp.arange(slots_total, dtype=jnp.int32) // MOST
    slot_hot = is_hot[slot_owner]

    def one_block(block_key):
        split_keys = jax.random.split(block_key, 2)
        ranks = jax.random.permutation(split_keys[0], slots_total).astype(jnp.int32)
        scores = slot_hot * slots_total + ranks
        chosen = lax.top_k(scores, ACT_DEV)[1].astype(jnp.int32)
        targets = chosen // MOST
        return jax.random.permutation(split_keys[1], targets).astype(jnp.int32)
    targets = jax.vmap(one_block)(jax.random.split(keys[1], DEVICES)).reshape(NACT)
    actives = jax.vmap(lambda pick_key: pick_distinct(pick_key, ACT_DEV))(jax.random.split(keys[2], DEVICES))
    actives = actives.at[0].set(pick_with_top(keys[3], ACT_DEV)).reshape(NACT)
    neighbours = jax.vmap(lambda pick_key: pick_distinct(pick_key, K))(jax.random.split(keys[4], NACT))
    neighbours = neighbours.at[0].set(pick_with_top(keys[5], K))
    return (targets, actives, neighbours)


def draw_assignment(key, part):
    targets, actives, neighbours = layout(jax.random.fold_in(key, 11))
    return targets[:, None]


def draw_active_index(key, part):
    targets, actives, neighbours = layout(jax.random.fold_in(key, 11))
    return actives


def draw_neighbour_index(key, part):
    targets, actives, neighbours = layout(jax.random.fold_in(key, 11))
    return neighbours


def draw_star_state(key, part):
    targets, actives, neighbours = layout(jax.random.fold_in(key, 11))
    keys = jax.random.split(jax.random.fold_in(key, 12), 5)
    spread = 0.25
    velocity = 0.5 * jax.random.normal(keys[3], (3, NSTARS), jnp.float32)
    centers = 2.0 * jax.random.normal(keys[0], (3, DEVICES), jnp.float32)
    star_owner = jnp.arange(NSTARS, dtype=jnp.int32) // S_DEV
    place = centers[:, star_owner] + spread * jax.random.normal(keys[1], (3, NSTARS), jnp.float32)
    active_owner = jnp.arange(NACT, dtype=jnp.int32) // ACT_DEV
    global_index = (active_owner * S_DEV + actives).astype(jnp.int32)
    active_place = centers[:, targets] + spread * jax.random.normal(keys[2], (3, NACT), jnp.float32)
    place = place.at[:, global_index].set(active_place)
    log_mass = jax.random.uniform(keys[4], (1, NSTARS), jnp.float32, math.log(0.3), math.log(3.0))
    masses = jnp.exp(log_mass) * (0.1 / K)
    return jnp.concatenate([place, velocity, masses]).astype(jnp.float32)


def block_levels(own_key, extent, shards, least, largest):
    def one(dim, blocks):
        steps = jax.random.uniform(jax.random.fold_in(jax.random.fold_in(own_key, 6), dim), (blocks,), jnp.float32, least / len(shards), largest / len(shards))
        return jnp.repeat(jnp.exp(steps), extent[dim] // blocks).reshape((-1,) + (1,) * (len(extent) - dim - 1))

    loudness = one(*shards[0])
    for cut in shards[1:]:
        loudness = loudness * one(*cut)
    return loudness


def bell_draw(stream_key, dims, width, bound, shards=(), kind=jnp.bfloat16):
    entries = width * jax.random.normal(stream_key, dims, jnp.float32)
    if shards:
        entries = entries * block_levels(stream_key, dims, shards, -0.22, 0.18)
    return jnp.clip(entries, -bound, bound).astype(kind)


def setup_inputs(seed: int = 0) -> dict:
    seeds = jax.random.split(jax.random.key(seed), 8)
    return {
        "star_state": draw_star_state(jax.random.fold_in(seeds[7], 71), 0),
        "active_index": draw_active_index(jax.random.fold_in(seeds[7], 71), 0),
        "neighbour_index": draw_neighbour_index(jax.random.fold_in(seeds[7], 71), 0),
        "assignment": draw_assignment(jax.random.fold_in(seeds[7], 71), 0),
        "start_state": bell_draw(seeds[4], (6, NACT), 1.0, 6.0, ((1, 32),), jnp.float32),
        "old_derivs": bell_draw(seeds[5], (6, NACT), 2.0, 12.0, ((1, 32),), jnp.float32),
        "step_size": jnp.clip(jnp.exp(math.log(1.0) - 2.3025851 * jax.random.uniform(seeds[6], (NACT,), jnp.float32) ** block_levels(seeds[6], (NACT,), ((0, 32),), -0.2, 0.2)), 0.1, 1.0),
    }


soft_sq = 0.01

def pair_terms(active_parts, other_parts):
    sep_x = other_parts[0] - active_parts[0]
    sep_y = other_parts[1] - active_parts[1]
    sep_z = other_parts[2] - active_parts[2]
    rel_x = other_parts[3] - active_parts[3]
    rel_y = other_parts[4] - active_parts[4]
    rel_z = other_parts[5] - active_parts[5]
    dist_sq = sep_x * sep_x + sep_y * sep_y + sep_z * sep_z + soft_sq
    inverse = 1.0 / dist_sq
    strength = other_parts[6] * inverse * jnp.sqrt(inverse)
    radial = 3.0 * (sep_x * rel_x + sep_y * rel_y + sep_z * rel_z) * inverse
    pieces = [strength * sep_x, strength * sep_y, strength * sep_z, strength * (rel_x - radial * sep_x), strength * (rel_y - radial * sep_y), strength * (rel_z - radial * sep_z)]
    return jnp.stack([lax.optimization_barrier(jnp.sum(term, axis=-1)) for term in pieces])

def hermite(total, start_state, old_derivs, step_size):
    half_step = step_size * 0.5
    twelfth = step_size * step_size / 12.0
    old_acc, old_jerk = (old_derivs[:3], old_derivs[3:])
    new_acc, new_jerk = (total[:3], total[3:])
    old_pos, old_vel = (start_state[:3], start_state[3:])
    new_vel = old_vel + (old_acc + new_acc) * half_step + (old_jerk - new_jerk) * twelfth
    new_pos = old_pos + (old_vel + new_vel) * half_step + (old_acc - new_acc) * twelfth
    return jnp.concatenate([new_pos, new_vel])

def reference(star_state, active_index, neighbour_index, assignment, start_state, old_derivs, step_size):
    owner_dev = jnp.arange(NACT, dtype=jnp.int32) // ACT_DEV
    global_index = (owner_dev * S_DEV + active_index).astype(jnp.int32)
    active_state = jnp.take(star_state[:6], global_index, axis=1)
    block_len = math.gcd(NACT, 64)
    block_count = NACT // block_len
    blocks = active_state.reshape(6, block_count, block_len).transpose(1, 0, 2)
    star_rows = [star_state[component][None, :] for component in range(7)]

    def one_block(block_state):
        return pair_terms([block_state[component][:, None] for component in range(6)], star_rows)
    total = lax.map(one_block, blocks).transpose(1, 0, 2).reshape(6, NACT)
    neighbour_global = (assignment[:, 0][:, None] * S_DEV + neighbour_index).astype(jnp.int32)
    tile_data = jnp.take(star_state, neighbour_global, axis=1)
    irregular = pair_terms([active_state[component][:, None] for component in range(6)], [tile_data[component] for component in range(7)])
    regular = total - irregular
    corrected = hermite(total, start_state, old_derivs, step_size)
    return (corrected, jnp.concatenate([regular, irregular]))
```

```python
import functools

import jax
import jax.numpy as jnp
from jax import lax
from jax.experimental import pallas as pl
from jax.experimental.pallas import tpu as pltpu
from jax.sharding import PartitionSpec as P

soft_sq = 0.01
LANES = 128
MESH = pl.DeviceIdType.MESH


def pair_sums(q, star, acc):
    dx, dy, dz = star[0] - q[0], star[1] - q[1], star[2] - q[2]
    ux, uy, uz = star[3] - q[3], star[4] - q[4], star[5] - q[5]
    s = dx * dx + dy * dy + dz * dz + soft_sq
    r = lax.rsqrt(s)
    inv = r * r
    w = (star[6] * r) * inv
    wk = w * ((dx * ux + dy * uy + dz * uz) * inv)
    return [
        acc[0] + w * dx,
        acc[1] + w * dy,
        acc[2] + w * dz,
        acc[3] + w * ux,
        acc[4] + w * uy,
        acc[5] + w * uz,
        acc[6] + wk * dx,
        acc[7] + wk * dy,
        acc[8] + wk * dz,
    ]


def lane_gather(load_tile, tiles, idx):
    low = idx % LANES
    high = idx // LANES
    out = jnp.zeros(idx.shape, jnp.float32)
    for t in range(tiles):
        got = jnp.take_along_axis(load_tile(t), low, axis=1)
        out = jnp.where(high == t, got, out)
    return out


def fill_states(star_ref, index_ref, q_ref):
    tiles = star_ref.shape[1] // LANES
    for part in range(index_ref.shape[1] // LANES):
        cols = slice(part * LANES, (part + 1) * LANES)
        idx = jnp.broadcast_to(index_ref[:, cols], (8, LANES))
        state = lane_gather(
            lambda t: star_ref[:, t * LANES : (t + 1) * LANES], tiles, idx
        )
        turned = jnp.transpose(state)
        for c in range(6):
            q_ref[c, cols, :] = jnp.broadcast_to(turned[:, c : c + 1], (LANES, LANES))


def rows_of(sums):
    actives = sums[0].shape[0]
    lane = lax.broadcasted_iota(jnp.int32, (actives, LANES), 1)
    wide = jnp.zeros((actives, LANES), jnp.float32)
    for c, col in enumerate(sums):
        wide = jnp.where(lane == c, jnp.broadcast_to(col, wide.shape), wide)
    return jnp.transpose(wide)[:8, :]


def total_kernel(axes, group, star_ref, index_ref, total_ref, slots, q_ref, acc_ref,
                 send_sem, recv_sem, own_sem):
    rows, cols = axes
    n = rows * cols
    me = lax.axis_index("row") * cols + lax.axis_index("col")
    actives = index_ref.shape[1]
    tiles = star_ref.shape[1] // LANES
    barrier = pltpu.get_barrier_semaphore()

    def place(k):
        other = lax.rem(me + k, n)
        return (lax.div(other, cols), lax.rem(other, cols))

    @pl.loop(1, n)
    def _(k):
        pl.semaphore_signal(barrier, inc=1, device_id=place(k), device_id_type=MESH)

    own = pltpu.make_async_copy(star_ref, slots.at[me], own_sem)
    own.start()
    fill_states(star_ref, index_ref, q_ref)
    acc_ref[...] = jnp.zeros_like(acc_ref)

    def add_block(block):
        @pl.loop(0, actives // (8 * group))
        def _(g):
            for sub in range(group):
                at = pl.ds(pl.multiple_of(g * (8 * group) + 8 * sub, 8), 8)
                q = [q_ref[c, at, :] for c in range(6)]
                acc = [acc_ref[c, at, :] for c in range(9)]
                for t in range(tiles):
                    lanes = slice(t * LANES, (t + 1) * LANES)
                    star = [jnp.broadcast_to(block[c : c + 1, lanes], (8, LANES)) for c in range(7)]
                    acc = pair_sums(q, star, acc)
                for c in range(9):
                    acc_ref[c, at, :] = acc[c]

    def copy(k):
        return pltpu.make_async_remote_copy(
            src_ref=star_ref, dst_ref=slots.at[me], send_sem=send_sem.at[k],
            recv_sem=recv_sem.at[k], device_id=place(k), device_id_type=MESH,
        )

    pl.semaphore_wait(barrier, n - 1)

    @pl.loop(1, n)
    def _(k):
        copy(k).start()

    add_block(star_ref)

    @pl.loop(1, n)
    def _(k):
        source = lax.rem(me + n - k, n)
        pltpu.make_async_remote_copy(
            src_ref=star_ref, dst_ref=slots.at[source], send_sem=send_sem.at[k],
            recv_sem=recv_sem.at[k], device_id=place(k), device_id_type=MESH,
        ).wait_recv()
        add_block(slots.at[source])

    @pl.loop(1, n)
    def _(k):
        copy(k).wait_send()

    own.wait()
    sums = [jnp.sum(acc_ref[c], axis=1, keepdims=True) for c in range(9)]
    jerk = [sums[3 + c] - 3.0 * sums[6 + c] for c in range(3)]
    total_ref[...] = rows_of(sums[:3] + jerk)


def finish_kernel(target_ref, every_ref, star_ref, index_ref, near_ref, total_ref, start_ref,
                  old_ref, step_ref, corrected_ref, forces_ref, q_ref, tile_ref, irr_ref):
    actives = index_ref.shape[1]
    tiles = star_ref.shape[1] // LANES
    fill_states(star_ref, index_ref, q_ref)

    @pl.loop(0, actives // 8)
    def _(g):
        base = pl.multiple_of(g * 8, 8)
        near = near_ref[pl.ds(base, 8), :]
        for i in range(8):
            block = every_ref.at[target_ref[base + i]]
            idx = jnp.broadcast_to(near[i : i + 1, :], (8, LANES))
            tile_ref[pl.ds(8 * i, 8), :] = lane_gather(
                lambda t: block[:, t * LANES : (t + 1) * LANES], tiles, idx
            )
        star = [tile_ref[pl.ds(c, 8, stride=8), :] for c in range(7)]
        q = [q_ref[c, pl.ds(base, 8), :] for c in range(6)]
        acc = pair_sums(q, star, [jnp.zeros((8, LANES), jnp.float32)] * 9)
        lane = lax.broadcasted_iota(jnp.int32, (8, LANES), 1)
        wide = jnp.zeros((8, LANES), jnp.float32)
        for c in range(3):
            wide = jnp.where(lane == c, jnp.sum(acc[c], axis=1, keepdims=True), wide)
            jerk = jnp.sum(acc[3 + c] - 3.0 * acc[6 + c], axis=1, keepdims=True)
            wide = jnp.where(lane == 3 + c, jerk, wide)
        irr_ref[pl.ds(base, 8), :] = wide

    irregular = jnp.transpose(irr_ref[...])[:6, :]
    total = total_ref[:6, :]
    forces_ref[0:6, :] = total - irregular
    forces_ref[6:12, :] = irregular
    h = step_ref[...]
    half = h * 0.5
    twelfth = h * h / 12.0
    a0, j0 = old_ref[0:3, :], old_ref[3:6, :]
    a1, j1 = total[0:3], total[3:6]
    x0, v0 = start_ref[0:3, :], start_ref[3:6, :]
    v1 = v0 + (a0 + a1) * half + (j0 - j1) * twelfth
    corrected_ref[0:3, :] = x0 + (v0 + v1) * half + (a0 - a1) * twelfth
    corrected_ref[3:6, :] = v1


def body(axes, star_state, active_index, neighbour_index, assignment, start_state, old_derivs, step_size):
    n = axes[0] * axes[1]
    stars = star_state.shape[1]
    actives = active_index.shape[0]
    vmem = pl.BlockSpec(memory_space=pltpu.VMEM)
    star8 = jnp.pad(star_state, ((0, 1), (0, 0)))
    index = active_index.reshape(1, actives)
    f32 = jnp.float32
    total, every = pl.pallas_call(
        functools.partial(total_kernel, axes, GROUP),
        out_shape=(jax.ShapeDtypeStruct((8, actives), f32), jax.ShapeDtypeStruct((n, 8, stars), f32)),
        in_specs=[vmem, vmem],
        out_specs=(vmem, vmem),
        scratch_shapes=[
            pltpu.VMEM((6, actives, LANES), f32),
            pltpu.VMEM((9, actives, LANES), f32),
            pltpu.SemaphoreType.DMA((n,)),
            pltpu.SemaphoreType.DMA((n,)),
            pltpu.SemaphoreType.DMA,
        ],
        compiler_params=pltpu.CompilerParams(collective_id=0, has_side_effects=True),
        name="total",
    )(star8, index)
    return pl.pallas_call(
        finish_kernel,
        out_shape=(jax.ShapeDtypeStruct((6, actives), f32), jax.ShapeDtypeStruct((12, actives), f32)),
        in_specs=[pl.BlockSpec(memory_space=pltpu.SMEM)] + [vmem] * 8,
        out_specs=(vmem, vmem),
        scratch_shapes=[
            pltpu.VMEM((6, actives, LANES), f32),
            pltpu.VMEM((64, LANES), f32),
            pltpu.VMEM((actives, LANES), f32),
        ],
        name="finish",
    )(assignment[:, 0], every, star8, index, neighbour_index, total, start_state, old_derivs,
      step_size.reshape(1, actives))


GROUP = 4


def solution(mesh):
    axes = (mesh.shape["row"], mesh.shape["col"])
    split = P(None, ("row", "col"))
    in_specs = (split, P(("row", "col")), P(("row", "col"), None), P(("row", "col"), None),
                split, split, P(("row", "col")))
    return jax.shard_map(functools.partial(body, axes), mesh=mesh, in_specs=in_specs,
                         out_specs=(split, split), check_vma=False)
```

```python
import functools

import jax
import jax.numpy as jnp
from jax import lax
from jax.experimental import pallas as pl
from jax.experimental.pallas import tpu as pltpu
from jax.sharding import PartitionSpec as P

soft_sq = 0.01
LANES = 128
TILE = 256
MESH = pl.DeviceIdType.MESH


def pair_sums(q, star, acc):
    dx, dy, dz = star[0] - q[0], star[1] - q[1], star[2] - q[2]
    ux, uy, uz = star[3] - q[3], star[4] - q[4], star[5] - q[5]
    s = dx * dx + dy * dy + dz * dz + soft_sq
    r = lax.rsqrt(s)
    inv = r * r
    w = (star[6] * r) * inv
    wk = w * ((dx * ux + dy * uy + dz * uz) * inv)
    return [
        acc[0] + w * dx,
        acc[1] + w * dy,
        acc[2] + w * dz,
        acc[3] + w * ux,
        acc[4] + w * uy,
        acc[5] + w * uz,
        acc[6] + wk * dx,
        acc[7] + wk * dy,
        acc[8] + wk * dz,
    ]


def lane_gather(load_tile, tiles, idx):
    low = idx % LANES
    high = idx // LANES
    out = jnp.zeros(idx.shape, jnp.float32)
    for t in range(tiles):
        got = jnp.take_along_axis(load_tile(t), low, axis=1)
        out = jnp.where(high == t, got, out)
    return out


def fill_states(star_ref, index_ref, q_ref):
    tiles = star_ref.shape[1] // LANES
    for part in range(index_ref.shape[1] // LANES):
        cols = slice(part * LANES, (part + 1) * LANES)
        idx = jnp.broadcast_to(index_ref[:, cols], (8, LANES))
        state = lane_gather(
            lambda t: star_ref[:, t * LANES : (t + 1) * LANES], tiles, idx
        )
        turned = jnp.transpose(state)
        for c in range(6):
            q_ref[c, cols, :] = jnp.broadcast_to(turned[:, c : c + 1], (LANES, LANES))


def rows_of(sums):
    actives = sums[0].shape[0]
    lane = lax.broadcasted_iota(jnp.int32, (actives, LANES), 1)
    wide = jnp.zeros((actives, LANES), jnp.float32)
    for c, col in enumerate(sums):
        wide = jnp.where(lane == c, jnp.broadcast_to(col, wide.shape), wide)
    return jnp.transpose(wide)[:8, :]


def split3(x):
    hi = x.astype(jnp.bfloat16).astype(jnp.float32)
    rest = x - hi
    mid = rest.astype(jnp.bfloat16).astype(jnp.float32)
    low = (rest - mid).astype(jnp.bfloat16).astype(jnp.float32)
    return hi, mid, low


def split2(x):
    hi = x.astype(jnp.bfloat16)
    return hi, (x - hi.astype(jnp.float32)).astype(jnp.bfloat16)


def total_kernel(axes, group, star_ref, index_ref, total_ref, slots, q_ref, qt_ref, qs_ref, star_parts,
                 act_parts, acc_ref, send_sem, recv_sem, own_sem):
    rows, cols = axes
    n = rows * cols
    me = lax.axis_index("row") * cols + lax.axis_index("col")
    actives = index_ref.shape[1]
    stars = star_ref.shape[1]
    barrier = pltpu.get_barrier_semaphore()
    f32 = jnp.float32

    def place(k):
        other = lax.rem(me + k, n)
        return (lax.div(other, cols), lax.rem(other, cols))

    @pl.loop(1, n)
    def _(k):
        pl.semaphore_signal(barrier, inc=1, device_id=place(k), device_id_type=MESH)

    own = pltpu.make_async_copy(star_ref, slots.at[me], own_sem)
    own.start()
    for part in range(actives // LANES):
        at = slice(part * LANES, (part + 1) * LANES)
        idx = jnp.broadcast_to(index_ref[:, at], (8, LANES))
        state = lane_gather(lambda t: star_ref[:, t * LANES : (t + 1) * LANES], stars // LANES, idx)
        qs_ref[:, at] = state
        turned = jnp.transpose(state)
        qt_ref[at, 0:8] = turned
        for c in range(3):
            q_ref[c, at, :] = jnp.broadcast_to(turned[:, c : c + 1], (LANES, TILE))
    acc_ref[...] = jnp.zeros_like(acc_ref)

    def add_block(block):
        center = block[:, 0:1]
        line = lax.broadcasted_iota(jnp.int32, (8, 1), 0)
        here = block[...] - center
        dots = jnp.sum(here[0:3] * here[3:6], axis=0, keepdims=True)
        here = jnp.where(line == 6, 1.0, jnp.where(line == 7, dots, here))
        hi, mid, low = split3(here)
        zero = jnp.zeros_like(hi)
        star_parts[...] = jnp.concatenate([hi, mid, low, hi, mid, hi, zero, zero], axis=0).astype(jnp.bfloat16)
        mine = qs_ref[...] - center
        both = jnp.sum(mine[0:3] * mine[3:6], axis=0, keepdims=True)
        side = jnp.concatenate([-mine[3:6], -mine[0:3], both, jnp.ones_like(both)], axis=0)
        hi, mid, low = split3(side)
        zero = jnp.zeros_like(hi)
        tall = jnp.concatenate([hi, hi, hi, mid, mid, low] + [zero] * 10, axis=0)
        act_parts[...] = jnp.transpose(tall)[:, :64].astype(jnp.bfloat16)
        shift = jnp.transpose(jnp.broadcast_to(center, (8, LANES)))[0:1, :]

        @pl.loop(0, actives // group)
        def _(g):
            at = pl.ds(pl.multiple_of(g * group, group), group)
            parts = [[], [], [], []]
            for t in range(stars // TILE):
                lanes = slice(t * TILE, (t + 1) * TILE)
                dv = jnp.dot(act_parts[at, :], star_parts[:, lanes], preferred_element_type=f32)
                pieces = [[], [], [], []]
                for sub in range(group // 16):
                    ra = pl.ds(pl.multiple_of(g * group + 16 * sub, 16), 16)
                    dx, dy, dz = [block[c : c + 1, lanes] - q_ref[c, ra, :] for c in range(3)]
                    s = dx * dx + dy * dy + dz * dz + soft_sq
                    r = lax.rsqrt(s)
                    inv = r * r
                    w = (block[6:7, lanes] * r) * inv
                    wk = w * (dv[16 * sub : 16 * sub + 16] * inv)
                    for i, p in enumerate(split2(w) + split2(wk)):
                        pieces[i].append(p)
                for i in range(4):
                    parts[i].append(jnp.concatenate(pieces[i], axis=0))
            full = [jnp.concatenate(p, axis=1) for p in parts]
            table = star_parts[0:32, :]

            def weigh(m):
                return lax.dot_general(m, table, (((1,), (1,)), ((), ())), preferred_element_type=f32)

            q = qt_ref[at, 0:8] - shift
            for i in range(2):
                out = weigh(full[2 * i]) + weigh(full[2 * i + 1])
                out = out[:, 0:8] + out[:, 8:16] + out[:, 16:24]
                acc_ref[i, at, :] += out - q * out[:, 6:7]

    def copy(k):
        return pltpu.make_async_remote_copy(
            src_ref=star_ref, dst_ref=slots.at[me], send_sem=send_sem.at[k],
            recv_sem=recv_sem.at[k], device_id=place(k), device_id_type=MESH,
        )

    pl.semaphore_wait(barrier, n - 1)

    @pl.loop(1, n)
    def _(k):
        copy(k).start()

    own.wait()

    @pl.loop(0, n)
    def _(k):
        source = lax.rem(me + n - k, n)

        @pl.when(k > 0)
        def _():
            pltpu.make_async_remote_copy(
                src_ref=star_ref, dst_ref=slots.at[source], send_sem=send_sem.at[k],
                recv_sem=recv_sem.at[k], device_id=place(k), device_id_type=MESH,
            ).wait_recv()

        add_block(slots.at[source])

    @pl.loop(1, n)
    def _(k):
        copy(k).wait_send()

    sums = [acc_ref[0, :, c : c + 1] for c in range(6)]
    jerk = [sums[3 + c] - 3.0 * acc_ref[1, :, c : c + 1] for c in range(3)]
    total_ref[...] = rows_of(sums[:3] + jerk)


def finish_kernel(target_ref, every_ref, star_ref, index_ref, near_ref, total_ref, start_ref,
                  old_ref, step_ref, corrected_ref, forces_ref, q_ref, tile_ref, irr_ref):
    actives = index_ref.shape[1]
    tiles = star_ref.shape[1] // LANES
    fill_states(star_ref, index_ref, q_ref)

    @pl.loop(0, actives // 8)
    def _(g):
        base = pl.multiple_of(g * 8, 8)
        near = near_ref[pl.ds(base, 8), :]
        for i in range(8):
            block = every_ref.at[target_ref[base + i]]
            idx = jnp.broadcast_to(near[i : i + 1, :], (8, LANES))
            tile_ref[pl.ds(8 * i, 8), :] = lane_gather(
                lambda t: block[:, t * LANES : (t + 1) * LANES], tiles, idx
            )
        star = [tile_ref[pl.ds(c, 8, stride=8), :] for c in range(7)]
        q = [q_ref[c, pl.ds(base, 8), :] for c in range(6)]
        acc = pair_sums(q, star, [jnp.zeros((8, LANES), jnp.float32)] * 9)
        lane = lax.broadcasted_iota(jnp.int32, (8, LANES), 1)
        wide = jnp.zeros((8, LANES), jnp.float32)
        for c in range(3):
            wide = jnp.where(lane == c, jnp.sum(acc[c], axis=1, keepdims=True), wide)
            jerk = jnp.sum(acc[3 + c] - 3.0 * acc[6 + c], axis=1, keepdims=True)
            wide = jnp.where(lane == 3 + c, jerk, wide)
        irr_ref[pl.ds(base, 8), :] = wide

    irregular = jnp.transpose(irr_ref[...])[:6, :]
    total = total_ref[:6, :]
    forces_ref[0:6, :] = total - irregular
    forces_ref[6:12, :] = irregular
    h = step_ref[...]
    half = h * 0.5
    twelfth = h * h / 12.0
    a0, j0 = old_ref[0:3, :], old_ref[3:6, :]
    a1, j1 = total[0:3], total[3:6]
    x0, v0 = start_ref[0:3, :], start_ref[3:6, :]
    v1 = v0 + (a0 + a1) * half + (j0 - j1) * twelfth
    corrected_ref[0:3, :] = x0 + (v0 + v1) * half + (a0 - a1) * twelfth
    corrected_ref[3:6, :] = v1


def body(axes, star_state, active_index, neighbour_index, assignment, start_state, old_derivs, step_size):
    n = axes[0] * axes[1]
    stars = star_state.shape[1]
    actives = active_index.shape[0]
    vmem = pl.BlockSpec(memory_space=pltpu.VMEM)
    star8 = jnp.pad(star_state, ((0, 1), (0, 0)))
    index = active_index.reshape(1, actives)
    f32 = jnp.float32
    total, every = pl.pallas_call(
        functools.partial(total_kernel, axes, GROUP),
        out_shape=(jax.ShapeDtypeStruct((8, actives), f32), jax.ShapeDtypeStruct((n, 8, stars), f32)),
        in_specs=[vmem, vmem],
        out_specs=(vmem, vmem),
        scratch_shapes=[
            pltpu.VMEM((3, actives, TILE), f32),
            pltpu.VMEM((actives, 8), f32),
            pltpu.VMEM((8, actives), f32),
            pltpu.VMEM((64, stars), jnp.bfloat16),
            pltpu.VMEM((actives, 64), jnp.bfloat16),
            pltpu.VMEM((2, actives, 8), f32),
            pltpu.SemaphoreType.DMA((n,)),
            pltpu.SemaphoreType.DMA((n,)),
            pltpu.SemaphoreType.DMA,
        ],
        compiler_params=pltpu.CompilerParams(collective_id=0, has_side_effects=True),
        name="total",
    )(star8, index)
    return pl.pallas_call(
        finish_kernel,
        out_shape=(jax.ShapeDtypeStruct((6, actives), f32), jax.ShapeDtypeStruct((12, actives), f32)),
        in_specs=[pl.BlockSpec(memory_space=pltpu.SMEM)] + [vmem] * 8,
        out_specs=(vmem, vmem),
        scratch_shapes=[
            pltpu.VMEM((6, actives, LANES), f32),
            pltpu.VMEM((64, LANES), f32),
            pltpu.VMEM((actives, LANES), f32),
        ],
        name="finish",
    )(assignment[:, 0], every, star8, index, neighbour_index, total, start_state, old_derivs,
      step_size.reshape(1, actives))


GROUP = 64


def solution(mesh):
    axes = (mesh.shape["row"], mesh.shape["col"])
    split = P(None, ("row", "col"))
    in_specs = (split, P(("row", "col")), P(("row", "col"), None), P(("row", "col"), None),
                split, split, P(("row", "col")))
    return jax.shard_map(functools.partial(body, axes), mesh=mesh, in_specs=in_specs,
                         out_specs=(split, split), check_vma=False)
```

```python
import functools

import jax
import jax.numpy as jnp
from jax import lax
from jax.experimental import pallas as pl
from jax.experimental.pallas import tpu as pltpu
from jax.sharding import PartitionSpec as P

soft_sq = 0.01
LANES = 128
WIDE = 4
TILE = 256
MESH = pl.DeviceIdType.MESH


def pair_sums(q, star, acc):
    dx, dy, dz = star[0] - q[0], star[1] - q[1], star[2] - q[2]
    ux, uy, uz = star[3] - q[3], star[4] - q[4], star[5] - q[5]
    s = dx * dx + dy * dy + dz * dz + soft_sq
    r = lax.rsqrt(s)
    inv = r * r
    w = (star[6] * r) * inv
    wk = w * ((dx * ux + dy * uy + dz * uz) * inv)
    return [
        acc[0] + w * dx,
        acc[1] + w * dy,
        acc[2] + w * dz,
        acc[3] + w * ux,
        acc[4] + w * uy,
        acc[5] + w * uz,
        acc[6] + wk * dx,
        acc[7] + wk * dy,
        acc[8] + wk * dz,
    ]


def lane_gather(load_tile, tiles, idx):
    low = idx % LANES
    high = idx // LANES
    out = jnp.zeros(idx.shape, jnp.float32)
    for t in range(tiles):
        got = jnp.take_along_axis(load_tile(t), low, axis=1)
        out = jnp.where(high == t, got, out)
    return out


def fill_states(star_ref, index_ref, q_ref):
    tiles = star_ref.shape[1] // LANES
    for part in range(index_ref.shape[1] // LANES):
        cols = slice(part * LANES, (part + 1) * LANES)
        idx = jnp.broadcast_to(index_ref[:, cols], (8, LANES))
        state = lane_gather(
            lambda t: star_ref[:, t * LANES : (t + 1) * LANES], tiles, idx
        )
        turned = jnp.transpose(state)
        for c in range(6):
            q_ref[c, cols, :] = jnp.broadcast_to(turned[:, c : c + 1], (LANES, LANES))


def rows_of(sums):
    actives = sums[0].shape[0]
    lane = lax.broadcasted_iota(jnp.int32, (actives, LANES), 1)
    wide = jnp.zeros((actives, LANES), jnp.float32)
    for c, col in enumerate(sums):
        wide = jnp.where(lane == c, jnp.broadcast_to(col, wide.shape), wide)
    return jnp.transpose(wide)[:8, :]


def split3(x):
    hi = x.astype(jnp.bfloat16).astype(jnp.float32)
    rest = x - hi
    mid = rest.astype(jnp.bfloat16).astype(jnp.float32)
    low = (rest - mid).astype(jnp.bfloat16).astype(jnp.float32)
    return hi, mid, low


def split2(x):
    hi = x.astype(jnp.bfloat16)
    return hi, (x - hi.astype(jnp.float32)).astype(jnp.bfloat16)


def total_kernel(axes, group, star_ref, index_ref, total_ref, slots, q_ref, qt_ref, qs_ref, star_parts, sum_parts,
                 act_parts, acc_ref, send_sem, recv_sem, own_sem):
    rows, cols = axes
    n = rows * cols
    me = lax.axis_index("row") * cols + lax.axis_index("col")
    actives = index_ref.shape[1]
    stars = star_ref.shape[1]
    barrier = pltpu.get_barrier_semaphore()
    f32 = jnp.float32

    def place(k):
        other = lax.rem(me + k, n)
        return (lax.div(other, cols), lax.rem(other, cols))

    @pl.loop(1, n)
    def _(k):
        pl.semaphore_signal(barrier, inc=1, device_id=place(k), device_id_type=MESH)

    own = pltpu.make_async_copy(star_ref, slots.at[me], own_sem)
    own.start()
    for part in range(actives // LANES):
        at = slice(part * LANES, (part + 1) * LANES)
        idx = jnp.broadcast_to(index_ref[:, at], (8, LANES))
        state = lane_gather(lambda t: star_ref[:, t * LANES : (t + 1) * LANES], stars // LANES, idx)
        qs_ref[:, at] = state
        turned = jnp.transpose(state)
        qt_ref[at, 0:8] = turned
        for c in range(3):
            q_ref[c, at, :] = jnp.broadcast_to(turned[:, c : c + 1], (LANES, TILE))
    acc_ref[...] = jnp.zeros_like(acc_ref)

    def add_block(block):
        center = block[:, 0:1]
        line = lax.broadcasted_iota(jnp.int32, (8, 1), 0)
        here = block[...] - center
        dots = jnp.sum(here[0:3] * here[3:6], axis=0, keepdims=True)
        here = jnp.where(line == 6, 1.0, jnp.where(line == 7, dots, here))
        hi, mid, low = split3(here)
        zero = jnp.zeros_like(hi)
        star_parts[...] = jnp.concatenate([hi, mid, low, hi, mid, hi, zero, zero], axis=0).astype(jnp.bfloat16)
        heavy = split3(here * block[6:7, :])
        sum_parts[...] = jnp.concatenate(list(heavy) + [zero], axis=0).astype(jnp.bfloat16)
        mine = qs_ref[...] - center
        both = jnp.sum(mine[0:3] * mine[3:6], axis=0, keepdims=True)
        side = jnp.concatenate([-mine[3:6], -mine[0:3], both, jnp.ones_like(both)], axis=0)
        hi, mid, low = split3(side)
        zero = jnp.zeros_like(hi)
        tall = jnp.concatenate([hi, hi, hi, mid, mid, low] + [zero] * 10, axis=0)
        act_parts[...] = jnp.transpose(tall)[:, :64].astype(jnp.bfloat16)
        shift = jnp.transpose(jnp.broadcast_to(center, (8, LANES)))[0:1, :]

        @pl.loop(0, actives // group)
        def _(g):
            at = pl.ds(pl.multiple_of(g * group, group), group)
            parts = [[], [], [], []]
            for t in range(stars // TILE):
                lanes = slice(t * TILE, (t + 1) * TILE)
                dv = jnp.dot(act_parts[at, :], star_parts[:, lanes], preferred_element_type=f32)
                pieces = [[], [], [], []]
                for sub in range(group // 16):
                    ra = pl.ds(pl.multiple_of(g * group + 16 * sub, 16), 16)
                    dx, dy, dz = [block[c : c + 1, lanes] - q_ref[c, ra, :] for c in range(3)]
                    s = dx * dx + dy * dy + dz * dz + soft_sq
                    r = lax.rsqrt(s)
                    inv = r * r
                    w = r * inv
                    wk = w * (dv[16 * sub : 16 * sub + 16] * inv)
                    for i, p in enumerate(split2(w) + split2(wk)):
                        pieces[i].append(p)
                for i in range(4):
                    parts[i].append(jnp.concatenate(pieces[i], axis=0))
            full = [jnp.concatenate(p, axis=1) for p in parts]
            table = sum_parts[...]

            def weigh(m):
                return lax.dot_general(m, table, (((1,), (1,)), ((), ())), preferred_element_type=f32)

            q = qt_ref[at, 0:8] - shift
            out = weigh(jnp.concatenate(full, axis=0))
            out = out[:, 0:8] + out[:, 8:16] + out[:, 16:24]
            for i in range(2):
                got = out[2 * i * group : (2 * i + 1) * group] + out[(2 * i + 1) * group : (2 * i + 2) * group]
                acc_ref[i, at, :] += got - q * got[:, 6:7]

    def copy(k):
        return pltpu.make_async_remote_copy(
            src_ref=star_ref, dst_ref=slots.at[me], send_sem=send_sem.at[k],
            recv_sem=recv_sem.at[k], device_id=place(k), device_id_type=MESH,
        )

    pl.semaphore_wait(barrier, n - 1)

    @pl.loop(1, n)
    def _(k):
        copy(k).start()

    own.wait()

    @pl.loop(0, n)
    def _(k):
        source = lax.rem(me + n - k, n)

        @pl.when(k > 0)
        def _():
            pltpu.make_async_remote_copy(
                src_ref=star_ref, dst_ref=slots.at[source], send_sem=send_sem.at[k],
                recv_sem=recv_sem.at[k], device_id=place(k), device_id_type=MESH,
            ).wait_recv()

        add_block(slots.at[source])

    @pl.loop(1, n)
    def _(k):
        copy(k).wait_send()

    sums = [acc_ref[0, :, c : c + 1] for c in range(6)]
    jerk = [sums[3 + c] - 3.0 * acc_ref[1, :, c : c + 1] for c in range(3)]
    total_ref[...] = rows_of(sums[:3] + jerk)


def finish_kernel(target_ref, every_ref, star_ref, index_ref, near_ref, total_ref, start_ref,
                  old_ref, step_ref, corrected_ref, forces_ref, q_ref, tile_ref, irr_ref):
    actives = index_ref.shape[1]
    tiles = star_ref.shape[1] // LANES
    fill_states(star_ref, index_ref, q_ref)

    @pl.loop(0, actives // (8 * WIDE))
    def _(g):
        lane = lax.broadcasted_iota(jnp.int32, (8, LANES), 1)
        for part in range(WIDE):
            base = pl.multiple_of((g * WIDE + part) * 8, 8)
            near = near_ref[pl.ds(base, 8), :]
            for i in range(8):
                block = every_ref.at[target_ref[base + i]]
                idx = jnp.broadcast_to(near[i : i + 1, :], (8, LANES))
                tile_ref[pl.ds(64 * part + 8 * i, 8), :] = lane_gather(
                    lambda t: block[:, t * LANES : (t + 1) * LANES], tiles, idx
                )
            star = [tile_ref[pl.ds(64 * part + c, 8, stride=8), :] for c in range(7)]
            q = [q_ref[c, pl.ds(base, 8), :] for c in range(6)]
            acc = pair_sums(q, star, [jnp.zeros((8, LANES), jnp.float32)] * 9)
            wide = jnp.zeros((8, LANES), jnp.float32)
            for c in range(3):
                wide = jnp.where(lane == c, jnp.sum(acc[c], axis=1, keepdims=True), wide)
                jerk = jnp.sum(acc[3 + c] - 3.0 * acc[6 + c], axis=1, keepdims=True)
                wide = jnp.where(lane == 3 + c, jerk, wide)
            irr_ref[pl.ds(base, 8), :] = wide

    irregular = jnp.transpose(irr_ref[...])[:6, :]
    total = total_ref[:6, :]
    forces_ref[0:6, :] = total - irregular
    forces_ref[6:12, :] = irregular
    h = step_ref[...]
    half = h * 0.5
    twelfth = h * h / 12.0
    a0, j0 = old_ref[0:3, :], old_ref[3:6, :]
    a1, j1 = total[0:3], total[3:6]
    x0, v0 = start_ref[0:3, :], start_ref[3:6, :]
    v1 = v0 + (a0 + a1) * half + (j0 - j1) * twelfth
    corrected_ref[0:3, :] = x0 + (v0 + v1) * half + (a0 - a1) * twelfth
    corrected_ref[3:6, :] = v1


def body(axes, star_state, active_index, neighbour_index, assignment, start_state, old_derivs, step_size):
    n = axes[0] * axes[1]
    stars = star_state.shape[1]
    actives = active_index.shape[0]
    vmem = pl.BlockSpec(memory_space=pltpu.VMEM)
    star8 = jnp.pad(star_state, ((0, 1), (0, 0)))
    index = active_index.reshape(1, actives)
    f32 = jnp.float32
    total, every = pl.pallas_call(
        functools.partial(total_kernel, axes, actives),
        out_shape=(jax.ShapeDtypeStruct((8, actives), f32), jax.ShapeDtypeStruct((n, 8, stars), f32)),
        in_specs=[vmem, vmem],
        out_specs=(vmem, vmem),
        scratch_shapes=[
            pltpu.VMEM((3, actives, TILE), f32),
            pltpu.VMEM((actives, 8), f32),
            pltpu.VMEM((8, actives), f32),
            pltpu.VMEM((64, stars), jnp.bfloat16),
            pltpu.VMEM((32, stars), jnp.bfloat16),
            pltpu.VMEM((actives, 64), jnp.bfloat16),
            pltpu.VMEM((2, actives, 8), f32),
            pltpu.SemaphoreType.DMA((n,)),
            pltpu.SemaphoreType.DMA((n,)),
            pltpu.SemaphoreType.DMA,
        ],
        compiler_params=pltpu.CompilerParams(collective_id=0, has_side_effects=True),
        name="total",
    )(star8, index)
    return pl.pallas_call(
        finish_kernel,
        out_shape=(jax.ShapeDtypeStruct((6, actives), f32), jax.ShapeDtypeStruct((12, actives), f32)),
        in_specs=[pl.BlockSpec(memory_space=pltpu.SMEM)] + [vmem] * 8,
        out_specs=(vmem, vmem),
        scratch_shapes=[
            pltpu.VMEM((6, actives, LANES), f32),
            pltpu.VMEM((64 * WIDE, LANES), f32),
            pltpu.VMEM((actives, LANES), f32),
        ],
        name="finish",
    )(assignment[:, 0], every, star8, index, neighbour_index, total, start_state, old_derivs,
      step_size.reshape(1, actives))


def solution(mesh):
    axes = (mesh.shape["row"], mesh.shape["col"])
    split = P(None, ("row", "col"))
    in_specs = (split, P(("row", "col")), P(("row", "col"), None), P(("row", "col"), None),
                split, split, P(("row", "col")))
    return jax.shard_map(functools.partial(body, axes), mesh=mesh, in_specs=in_specs,
                         out_specs=(split, split), check_vma=False)
```
